32 devices in a mesh: cube: 2 (over x), chan: 8 (over z, y), split: 2 (over core).
Axes of the slice: x: 2, y: 2, z: 4, core: 2. Of those that a mesh axis runs over, the one named last changes fastest.
Arguments:
- sky_image: bfloat16 [16, 8, 1, 2, 512, 128], P(('cube', 'chan'), None, None, 'split'), parts along dimension 0, may hold values from 0 to 8
- dirty_image: bfloat16 [16, 8, 1, 2, 512, 128], P(('cube', 'chan'), None, None, 'split'), parts along dimension 0, may hold values from -6 to 6
- uv_weights: int32 [16, 1024, 512], P(('cube', 'chan'), 'split'), parts along dimension 0, may hold values from 0 to 7
- dual_coeffs: bfloat16 [4, 16, 8, 2, 512, 128], P(None, 'cube', 'chan', 'split'), parts along dimension 1, may hold values from -3 to 3
- support_mask: int32 [8, 2, 512, 128], P('chan', 'split'), may hold values 0 or 1
- row_taps: float32 [4, 17], replicated, may hold values from -1.5 to 1.5
- col_taps: float32 [4, 17], replicated, may hold values from -1.5 to 1.5
Outputs:
- new_image: bfloat16 [16, 8, 1, 2, 512, 128], P(('cube', 'chan'), None, None, 'split'), parts along dimension 0
- new_dual: bfloat16 [4, 16, 8, 2, 512, 128], P(None, 'cube', 'chan', 'split'), parts along dimension 1
The draws below stay inside these ranges and needn't reach their ends.
There are 2 independent parts, one for each index of `cube`. The reference program is written for one: setup_inputs(seed, part) draws one part's arguments, and reference() takes and returns one part's arrays. A program takes and returns all parts, laid end to end along the dimension named above; an argument that names none is the same for every part. Nothing has to cross between parts.
All inputs are finite; a program needn't handle non-finite values. No bound on the sum of `support_mask` on one device may be relied on, other than what follows from the above.
Results may differ from the reference program's by a relative error of at most 0.015.
Values may be sent and summed in bfloat16 or wider, within the bound.
A program may use at most 128 MiB of HBM per device.

```python
import math
import jax
import jax.numpy as jnp
from jax import lax

NPIX = 1024
FCOLS = 8
NB = 4
MARGIN = 8
TAPS = 17
CH = 8
FACETS = 8
FROWS = 1
FS = 128
SR = 512
HALF = 512


def draw_sky_image(key, part):
    full_shape = (CH, FCOLS, FROWS, 2, SR, FS)
    key_space = jax.random.fold_in(key, 12)
    key_fresh = jax.random.fold_in(key, 13)
    key_jitter = jax.random.fold_in(key, 14)
    channel_ramp = jnp.arange(CH, dtype=jnp.float32) / max(CH - 1, 1)
    fresh = jax.random.uniform(key_fresh, full_shape, jnp.float32, 0.0, 2.0)
    jitter = jnp.exp(jax.random.uniform(key_jitter, (CH,), jnp.float32, -0.2, 0.2))
    channel_scale = 0.15 * jnp.exp(channel_ramp * math.log(10.0)) * jitter
    spatial = jnp.exp(jax.random.uniform(key_space, full_shape[1:], jnp.float32, -math.log(3.0), math.log(3.0)))
    values = channel_scale[:, None, None, None, None, None] * spatial[None] * fresh
    return jnp.minimum(values, 8.0).astype(jnp.bfloat16)


def place_ends(result, own_key, smallest, largest):
    dims = result.shape
    spot = [jax.random.randint(jax.random.fold_in(own_key, axis), (), 0, dims[axis]) for axis in range(len(dims))]
    result = result.at[tuple(spot)].set(smallest)
    longest = dims.index(max(dims))
    spot[longest] = (spot[longest] + 1) % dims[longest]
    return result.at[tuple(spot)].set(largest)


def block_scale(stream_key, dims, pieces, low, largest):
    factor_of, own = 1.0, jax.random.fold_in(stream_key, 6)
    for axis_at, shards_of in pieces:
        heights = jnp.exp(jax.random.uniform(jax.random.fold_in(own, axis_at), (shards_of,), jnp.float32, low / len(pieces), largest / len(pieces)))
        factor_of = factor_of * jnp.repeat(heights, dims[axis_at] // shards_of).reshape([-1 if axis == axis_at else 1 for axis in range(len(dims))])
    return factor_of


def centred(stream_key, shape, scale, reach, shards=(), kind=jnp.bfloat16):
    entries = jax.random.normal(stream_key, shape, jnp.float32) * scale
    if len(shards) > 0:
        entries = block_scale(stream_key, shape, shards, -0.22, 0.18) * entries
    return jnp.clip(entries, min=-reach, max=reach).astype(kind)


def setup_inputs(seed: int = 0, part: int = 0) -> dict:
    streams_of = jax.random.split(jax.random.key(seed), 8)
    part_keys = jax.random.split(jax.random.fold_in(streams_of[7], part), 8)
    sky_image = draw_sky_image(jax.random.fold_in(jax.random.fold_in(streams_of[7], part), 71), part)
    dirty_image = centred(part_keys[1], (CH, FCOLS, FROWS, 2, SR, FS), 1.0, 6.0, ((0, 8), (3, 2)))
    uv_weights = place_ends(jax.random.randint(part_keys[2], (CH, NPIX, HALF), 0, 8), jax.random.fold_in(part_keys[2], 1), 0, 7).astype(jnp.int32)
    dual_coeffs = centred(part_keys[3], (NB, CH, FACETS, 2, SR, FS), 0.5, 3.0, ((2, 8), (3, 2)))
    support_mask = place_ends((jax.random.randint(streams_of[4], (FACETS, 2, SR, FS), 0, 4) < 3).astype(jnp.int32), jax.random.fold_in(streams_of[4], 1), 0, 1)
    row_taps = centred(streams_of[5], (NB, TAPS), TAPS ** -0.5, 1.5, (), jnp.float32)
    col_taps = centred(streams_of[6], (NB, TAPS), TAPS ** -0.5, 1.5, (), jnp.float32)
    return dict(sky_image=sky_image, dirty_image=dirty_image, uv_weights=uv_weights, dual_coeffs=dual_coeffs, support_mask=support_mask, row_taps=row_taps, col_taps=col_taps)


primal_step = 0.5
dual_step = 0.5
radius = 6.0
weight_unit = 0.25

def dft_block(out_rows, in_rows):
    product = out_rows[:, None] * in_rows[None, :] % NPIX
    phases = product.astype(jnp.float32) * (2.0 * math.pi / NPIX)
    factor = 1.0 / math.sqrt(NPIX)
    return ((jnp.cos(phases) * factor).astype(jnp.bfloat16), (-jnp.sin(phases) * factor).astype(jnp.bfloat16))

def to_full(blocks, leading):
    count = len(leading)
    shaped = blocks.reshape(leading + (FCOLS, FROWS, 2, SR, FS))
    axes_order = tuple(range(count)) + (count + 1, count + 2, count + 3, count, count + 4)
    return shaped.transpose(axes_order).reshape(leading + (NPIX, NPIX))

def from_full(full, leading, target):
    count = len(leading)
    shaped = full.reshape(leading + (FROWS, 2, SR, FCOLS, FS))
    axes_order = tuple(range(count)) + (count + 3, count, count + 1, count + 2, count + 4)
    return shaped.transpose(axes_order).reshape(target)

def filter_axis(values, tap_values, axis, adjoint):
    as_float = values.astype(jnp.float32)
    padding = [(0, 0)] * as_float.ndim
    padding[axis] = (MARGIN, MARGIN)
    padded = jnp.pad(as_float, padding)
    extent = as_float.shape[axis]
    summed = jnp.zeros_like(as_float)
    for tap_index in range(TAPS):
        offset = 2 * MARGIN - tap_index if adjoint else tap_index
        summed = summed + tap_values[tap_index].astype(jnp.float32) * lax.slice_in_dim(padded, offset, offset + extent, axis=axis)
    return summed

def reference(sky_image, dirty_image, uv_weights, dual_coeffs, support_mask, row_taps, col_taps):
    pixel_index = jnp.arange(NPIX, dtype=jnp.int32)
    freq_index = jnp.arange(HALF, dtype=jnp.int32)
    cx_re, cx_im = dft_block(freq_index, pixel_index)
    cy_re, cy_im = dft_block(pixel_index, pixel_index)

    def channel_gradient(pair):
        picture, counts = pair
        half_re = jnp.dot(picture, cx_re.T, preferred_element_type=jnp.float32).astype(jnp.bfloat16)
        half_im = jnp.dot(picture, cx_im.T, preferred_element_type=jnp.float32).astype(jnp.bfloat16)
        vis_re = jnp.dot(cy_re, half_re, preferred_element_type=jnp.float32) - jnp.dot(cy_im, half_im, preferred_element_type=jnp.float32)
        vis_im = jnp.dot(cy_re, half_im, preferred_element_type=jnp.float32) + jnp.dot(cy_im, half_re, preferred_element_type=jnp.float32)
        weight_scale = weight_unit * counts.astype(jnp.float32)
        res_re = (weight_scale * vis_re).astype(jnp.bfloat16)
        res_im = (weight_scale * vis_im).astype(jnp.bfloat16)
        back_re = (jnp.dot(cy_re.T, res_re, preferred_element_type=jnp.float32) + jnp.dot(cy_im.T, res_im, preferred_element_type=jnp.float32)).astype(jnp.bfloat16)
        back_im = (jnp.dot(cy_re.T, res_im, preferred_element_type=jnp.float32) - jnp.dot(cy_im.T, res_re, preferred_element_type=jnp.float32)).astype(jnp.bfloat16)
        return jnp.dot(back_re, cx_re, preferred_element_type=jnp.float32) + jnp.dot(back_im, cx_im, preferred_element_type=jnp.float32)
    picture = to_full(sky_image, (CH,))
    dirty = to_full(dirty_image, (CH,)).astype(jnp.float32)
    gradient = lax.map(channel_gradient, (picture, uv_weights))
    row_bf = row_taps.astype(jnp.bfloat16)
    col_bf = col_taps.astype(jnp.bfloat16)
    dual_full = to_full(dual_coeffs, (NB, CH))
    adjoint = jnp.zeros((CH, NPIX, NPIX), jnp.float32)
    for basis in range(NB):
        along = filter_axis(dual_full[basis], col_bf[basis], 2, True).astype(jnp.bfloat16)
        adjoint = adjoint + filter_axis(along, row_bf[basis], 1, True)
    adjoint_rounded = lax.optimization_barrier(adjoint.astype(jnp.bfloat16)).astype(jnp.float32)
    updated = jnp.maximum(picture.astype(jnp.float32) - primal_step * (gradient - dirty + adjoint_rounded), 0.0)
    new_full = updated.astype(jnp.bfloat16)
    extrapolated = (2.0 * new_full.astype(jnp.float32) - picture.astype(jnp.float32)).astype(jnp.bfloat16)
    keep_mask = to_full(support_mask, ()).astype(jnp.float32)
    duals = []
    for basis in range(NB):
        along = filter_axis(extrapolated, col_bf[basis], 2, False).astype(jnp.bfloat16)
        coefficients = filter_axis(along, row_bf[basis], 1, False)
        stepped = dual_full[basis].astype(jnp.float32) + dual_step * coefficients
        length = jnp.sqrt(lax.optimization_barrier(jnp.sum(stepped * stepped, axis=0)))
        shrink = radius * keep_mask / jnp.maximum(length, radius)
        duals.append((stepped * shrink[None]).astype(jnp.bfloat16))
    new_dual = from_full(jnp.stack(duals), (NB, CH), (NB, CH, FACETS, 2, SR, FS))
    new_image = from_full(new_full, (CH,), (CH, FCOLS, FROWS, 2, SR, FS))
    return (new_image, new_dual)
```

```python
import functools
import math

import jax
import jax.numpy as jnp
from jax import lax
from jax.experimental import pallas as pl
from jax.experimental.pallas import tpu as pltpu
from jax.sharding import PartitionSpec as P

NB = 4
TAPS = 17
MARGIN = 8
PAD = 16

primal_step = 0.5
dual_step = 0.5
radius = 6.0
weight_unit = 0.25
f32 = jnp.float32
bf16 = jnp.bfloat16


def dot(a, b):
    return jnp.dot(a, b, preferred_element_type=f32)


def col_dft(npix):
    half = npix // 2
    product = jnp.arange(npix)[:, None] * jnp.arange(half)[None, :] % npix
    phases = product.astype(f32) * (2.0 * math.pi / npix)
    factor = 1.0 / math.sqrt(npix)
    return jnp.concatenate(
        [(jnp.cos(phases) * factor).astype(bf16), (-jnp.sin(phases) * factor).astype(bf16)], axis=1
    )


def side_cols(k, width):
    return jnp.where(k < MARGIN, k - MARGIN, width - MARGIN + k)


def toeplitz(taps, index):
    out = jnp.zeros((NB,) + index.shape, f32)
    for t in range(TAPS):
        out = jnp.where(index[None] == t, taps[:, t][:, None, None], out)
    return out


def adjoint_tables(row_taps, col_taps, width, block):
    h = row_taps.astype(bf16).astype(f32)
    g = col_taps.astype(bf16).astype(f32)
    i = jnp.arange(width)[:, None]
    j = jnp.arange(width)[None, :]
    main = toeplitz(g, j - i + MARGIN)
    k = jnp.arange(width)[None, :]
    side_index = jnp.where(k < 2 * MARGIN, side_cols(k, width) - i + MARGIN, -1)
    side = toeplitz(g, side_index)
    cols = jnp.concatenate([main, side], axis=2).astype(bf16)
    r = jnp.arange(block)[:, None]
    w = jnp.arange(NB * (block + 2 * PAD))[None, :]
    span = block + 2 * PAD
    rows = jnp.zeros((block, NB * span), f32)
    index = r - w % span + PAD + MARGIN
    for t in range(TAPS):
        tap_row = jnp.repeat(h[:, t], span)[None, :]
        rows = jnp.where(index == t, tap_row, rows)
    return cols, rows.astype(bf16)


def forward_tables(row_taps, col_taps, width, block):
    h = row_taps.astype(bf16).astype(f32)
    g = col_taps.astype(bf16).astype(f32)
    i = jnp.arange(width)[:, None]
    j = jnp.arange(NB * width)[None, :]
    main_index = i - j % width + MARGIN
    side_index = jnp.where(i < 2 * MARGIN, side_cols(i, width) - j % width + MARGIN, -1)
    index = jnp.concatenate([main_index, side_index], axis=0)
    cols = jnp.zeros(index.shape, f32)
    for t in range(TAPS):
        tap_row = jnp.repeat(g[:, t], width)[None, :]
        cols = jnp.where(index == t, tap_row, cols)
    r = jnp.arange(block)[:, None]
    w = jnp.arange(block + 2 * PAD)[None, :]
    rows = toeplitz(h, w - r - PAD + MARGIN)
    return cols.astype(bf16), rows.astype(bf16)


def spill_tables(fcols, width):
    span = 2 * MARGIN
    row = jnp.arange(fcols * span)[:, None]
    col = jnp.arange(fcols * width)[None, :]
    rb, rk = row // span, row % span
    gather = jnp.where(rk >= MARGIN, (rb + 1) * width + rk - MARGIN, rb * width - MARGIN + rk)
    table = (gather == col).astype(bf16)
    return table


def adjoint_body(C, R, W, B, u, up, lo, gcols, hrows, adj, adjs, dc, dcs):
    per = W // (2 * MARGIN)
    for n in range(NB):
        main = gcols[n, :, :W]
        side0 = gcols[n, :, W:].astype(f32)
        for c0 in range(0, C, per):
            acc = None
            for cc in range(per):
                c = c0 + cc
                side = pltpu.roll(side0, 2 * MARGIN * cc, 1) if cc else side0
                table = jnp.concatenate([main, side.astype(bf16)], axis=1)
                rows = jnp.concatenate([up[n, c], u[n, c], lo[n, c]], axis=0)
                out = dot(rows, table)
                dc[n, :, c * W : (c + 1) * W] = out[:, :W].astype(bf16)
                acc = out[:, W:] if acc is None else acc + out[:, W:]
            dcs[n, :, c0 * 2 * MARGIN : c0 * 2 * MARGIN + W] = acc.astype(bf16)
    span = B + 2 * PAD
    for k in range(R // B):
        lo_row = k * B
        hr = hrows[...]
        for c in range(0, C, 2):
            win = jnp.concatenate(
                [dc[n, lo_row : lo_row + span, c * W : (c + 2) * W] for n in range(NB)], axis=0
            )
            out = dot(hr, win).astype(bf16)
            adj[c, lo_row : lo_row + B] = out[:, :W]
            adj[c + 1, lo_row : lo_row + B] = out[:, W:]
        for c0 in range(0, C, per):
            lanes = c0 * 2 * MARGIN
            win = jnp.concatenate(
                [dcs[n, lo_row : lo_row + span, lanes : lanes + W] for n in range(NB)], axis=0
            )
            out = dot(hr, win).T.astype(bf16)
            for cc in range(per):
                adjs[c0 + cc, :, lo_row : lo_row + B] = out[cc * 16 : cc * 16 + 16]


def half_body(FC, W, x, colT, out):
    full = out.shape[1]
    rows = jnp.concatenate([x[b] for b in range(FC)], axis=1)

    @pl.loop(0, full // 256)
    def _(j):
        lanes = pl.ds(pl.multiple_of(j * 256, 256), 256)
        out[:, lanes] = dot(rows, colT[:, lanes]).astype(bf16)


def table_body(s, FR, R, colT, bown, aown, aoth):
    half = FR * R
    for a in range(FR):
        own = pl.ds(pl.multiple_of((2 * a + s) * R, R), R)
        bown[a * R : (a + 1) * R] = colT[own, :]
    sign_row = lax.broadcasted_iota(jnp.int32, (1, half), 1) % 2
    flip = jnp.where((sign_row == 1) & (s == 1), -1.0, 1.0).astype(f32)
    for dst, part in ((aown, s), (aoth, 1 - s)):
        for q in range(2):
            pieces = [
                colT[pl.ds(pl.multiple_of((2 * a + part) * R, R), R), q * half : (q + 1) * half]
                for a in range(FR)
            ]
            block = jnp.concatenate(pieces, axis=0) if FR > 1 else pieces[0]
            dst[:, q * half : (q + 1) * half] = (block.astype(f32).T * flip).astype(bf16)


def stack_re_im(ref, lanes_re, lanes_im, transpose):
    re, im = ref[:, lanes_re], ref[:, lanes_im]
    if transpose:
        return jnp.concatenate([re, im], 0), jnp.concatenate([im, -re], 0)
    return jnp.concatenate([re, -im], 0), jnp.concatenate([im, re], 0)


def vis_body(half, aown, aoth, hown, hoth, wts, out):
    step = 256

    @pl.loop(0, half // step)
    def _(j):
        re_l = pl.ds(pl.multiple_of(j * step, step), step)
        im_l = pl.ds(pl.multiple_of(j * step + half, step), step)
        own_re, own_im = stack_re_im(hown, re_l, im_l, False)
        oth_re, oth_im = stack_re_im(hoth, re_l, im_l, False)
        scale = weight_unit * wts[:, re_l].astype(f32)
        re = dot(aown[...], own_re) + dot(aoth[...], oth_re)
        out[:, re_l] = (scale * re).astype(bf16)
        im = dot(aown[...], own_im) + dot(aoth[...], oth_im)
        out[:, im_l] = (scale * im).astype(bf16)


def back_body(s, half, bown, wown, woth, out):
    step = 256
    odd = lax.broadcasted_iota(jnp.int32, (half, 1), 0) % 2 == 1
    own_sign = jnp.where(odd & (s == 1), -1.0, 1.0)
    oth_sign = jnp.where(odd & (s == 0), -1.0, 1.0)

    @pl.loop(0, half // step)
    def _(j):
        re_l = pl.ds(pl.multiple_of(j * step, step), step)
        im_l = pl.ds(pl.multiple_of(j * step + half, step), step)
        own_re, own_im = stack_re_im(wown, re_l, im_l, True)
        oth_re, oth_im = stack_re_im(woth, re_l, im_l, True)
        re = own_sign * dot(bown[...], own_re) + oth_sign * dot(bown[...], oth_re)
        out[:, re_l] = re.astype(bf16)
        im = own_sign * dot(bown[...], own_im) + oth_sign * dot(bown[...], oth_im)
        out[:, im_l] = im.astype(bf16)


def image_body(FC, FR, R, W, back, colT, spill, x, d, adj, adjs, new, ext, exts):
    st_rows = []
    for a in range(FR):
        parts = jnp.concatenate([adjs[b * FR + a] for b in range(FC)], axis=0)
        st_rows.append(parts.astype(f32).T.astype(bf16))
    st = jnp.concatenate(st_rows, axis=0) if FR > 1 else st_rows[0]
    es = None
    for b in range(FC):
        cols = slice(b * W, (b + 1) * W)
        grad = lax.dot_general(
            back[...], colT[cols, :], (((1,), (1,)), ((), ())), preferred_element_type=f32
        )
        grad = grad + dot(st, spill[:, cols])
        pieces = [adj[b * FR + a] for a in range(FR)]
        main = jnp.concatenate(pieces, axis=0) if FR > 1 else pieces[0]
        xb = x[b].astype(f32)
        upd = xb - primal_step * (grad - d[b].astype(f32) + main.astype(f32))
        nb = jnp.maximum(upd, 0.0).astype(bf16)
        eb = (2.0 * nb.astype(f32) - xb).astype(bf16)
        new[b] = nb
        for a in range(FR):
            ext[b * FR + a] = eb[a * R : (a + 1) * R]
        part = lax.dot_general(
            eb, spill[:, cols], (((1,), (1,)), ((), ())), preferred_element_type=f32
        )
        es = part if es is None else es + part
    for a in range(FR):
        t = es[a * R : (a + 1) * R].T.astype(bf16)
        for b in range(FC):
            exts[b * FR + a] = t[b * 16 : b * 16 + 16]


def forward_cols_body(C, R, W, main, sides, fcols, ic):
    per = W // 16
    for c0 in range(0, C, per):
        parts = jnp.concatenate([sides[c0 + cc] for cc in range(per)], axis=0)
        st = parts.astype(f32).T.astype(bf16)
        for cc in range(per):
            c = c0 + cc
            zeros_a = jnp.zeros((cc * 16, NB * W), bf16)
            zeros_b = jnp.zeros((W - 16 - cc * 16, NB * W), bf16)
            pieces = [fcols[:W], fcols[W : W + 16]]
            if cc:
                pieces.insert(1, zeros_a)
            if cc < per - 1:
                pieces.append(zeros_b)
            table = jnp.concatenate(pieces, axis=0)
            out = dot(jnp.concatenate([main[c], st], axis=1), table)
            for n in range(NB):
                ic[n, PAD : PAD + R, c * W : (c + 1) * W] = out[:, n * W : (n + 1) * W].astype(bf16)


def shrink_body(C, R, W, B, ic, frows, u, mask, out):
    span = B + 2 * PAD
    for k in range(R // B):
        keep = radius * mask[k * B : (k + 1) * B].astype(f32)
        for n in range(NB):
            hr = frows[n]
            coef = dot(hr, ic[n, k * B : k * B + span])
            total = None
            steps = []
            for c in range(C):
                st = u[n, c, k * B : (k + 1) * B].astype(f32) + dual_step * coef[:, c * W : (c + 1) * W]
                steps.append(st)
                total = st * st if total is None else total + st * st
            scale = keep / jnp.maximum(jnp.sqrt(total), radius)
            for c in range(C):
                out[n, c, k * B : (k + 1) * B] = (steps[c] * scale).astype(bf16)


def call(body, outs, scratch=(), flops=10**9):
    params = pltpu.CompilerParams(vmem_limit_bytes=60 * 2**20)
    return pl.pallas_call(
        body,
        out_shape=[jax.ShapeDtypeStruct(o, bf16) for o in outs],
        scratch_shapes=[pltpu.VMEM(x, bf16) for x in scratch],
        compiler_params=params,
        cost_estimate=pl.CostEstimate(flops=flops, bytes_accessed=4 * 2**20, transcendentals=0),
    )


def per_device(sky_image, dirty_image, uv_weights, dual_coeffs, support_mask, row_taps, col_taps):
    FC, FR = sky_image.shape[1], sky_image.shape[2]
    R, W = sky_image.shape[4], sky_image.shape[5]
    C = dual_coeffs.shape[1]
    npix = FC * W
    half = npix // 2
    B = min(128, R)
    RP = R + 2 * PAD
    s = lax.axis_index("split")
    u = dual_coeffs.reshape(NB, C, R, W)
    x = sky_image.reshape(FC, FR * R, W)
    d = dirty_image.reshape(FC, FR * R, W)
    wts = uv_weights.reshape(half, half)
    mask = support_mask.reshape(R, W)
    colT = col_dft(npix)
    spill = spill_tables(FC, W)
    chain = ("chan", "split")
    count = lax.axis_size(chain)
    down = [(i, i + 1) for i in range(count) if (i + 1) % (2 * FR)]
    upward = [(i + 1, i) for i in range(count) if (i + 1) % (2 * FR)]
    swap = [(0, 1), (1, 0)]

    up = lax.ppermute(u[:, :, R - PAD :], chain, down)
    lo = lax.ppermute(u[:, :, :PAD], chain, upward)
    gcols, hrows = adjoint_tables(row_taps, col_taps, W, B)
    adj, adjs = call(
        functools.partial(adjoint_body, C, R, W, B),
        [(C, R, W), (C, 16, R)],
        [(NB, RP, C * W), (NB, RP, C * 16)],
    )(u, up, lo, gcols, hrows)
    adj = lax.all_to_all(adj, "chan", 0, 0, tiled=True)
    adjs = lax.all_to_all(adjs, "chan", 0, 0, tiled=True)

    (hown,) = call(functools.partial(half_body, FC, W), [(half, npix)])(x, colT)
    hoth = lax.ppermute(hown, "split", swap)

    def tables(colT_ref, bown, aown, aoth):
        table_body(lax.axis_index("split"), FR, R, colT_ref, bown, aown, aoth)

    bown, aown, aoth = call(tables, [(half, npix)] * 3)(colT)
    (wown,) = call(functools.partial(vis_body, half), [(half, npix)])(aown, aoth, hown, hoth, wts)
    woth = lax.ppermute(wown, "split", swap)

    def back_call(*refs):
        back_body(lax.axis_index("split"), half, *refs)

    (back,) = call(back_call, [(half, npix)])(bown, wown, woth)
    new, ext, exts = call(
        functools.partial(image_body, FC, FR, R, W),
        [(FC, FR * R, W), (C, R, W), (C, 16, R)],
    )(back, colT, spill, x, d, adj, adjs)
    main = lax.all_to_all(ext, "chan", 0, 0, tiled=True)
    sides = lax.all_to_all(exts, "chan", 0, 0, tiled=True)
    fcols, frows = forward_tables(row_taps, col_taps, W, B)

    def fcall(main, sides, fcols, ic):
        forward_cols_body(C, R, W, main, sides, fcols, ic)

    (ic,) = call(fcall, [(NB, RP, C * W)])(main, sides, fcols)
    top = lax.ppermute(ic[:, R : R + PAD], chain, down)
    bottom = lax.ppermute(ic[:, PAD : 2 * PAD], chain, upward)

    def scall(ic, top, bottom, frows, u, mask, out, ics):
        ics[:, :PAD] = top[...]
        ics[:, PAD : PAD + R] = ic[:, PAD : PAD + R]
        ics[:, PAD + R :] = bottom[...]
        shrink_body(C, R, W, B, ics, frows, u, mask, out)

    (new_dual,) = call(scall, [(NB, C, R, W)], [(NB, RP, C * W)])(ic, top, bottom, frows, u, mask)
    return (new.reshape(sky_image.shape), new_dual.reshape(dual_coeffs.shape))


def solution(mesh):
    placed = (
        P(("cube", "chan"), None, None, "split", None, None),
        P(("cube", "chan"), None, None, "split", None, None),
        P(("cube", "chan"), "split", None),
        P(None, "cube", "chan", "split", None, None),
        P("chan", "split", None, None),
        P(),
        P(),
    )
    return jax.shard_map(
        per_device,
        mesh=mesh,
        in_specs=placed,
        out_specs=(
            P(("cube", "chan"), None, None, "split", None, None),
            P(None, "cube", "chan", "split", None, None),
        ),
        check_vma=False,
    )
```

```python
import functools
import math

import jax
import jax.numpy as jnp
import numpy as np
from jax import lax
from jax.experimental import pallas as pl
from jax.experimental.pallas import tpu as pltpu
from jax.sharding import PartitionSpec as P

NB = 4
TAPS = 17
MARGIN = 8
PAD = 16

primal_step = 0.5
dual_step = 0.5
radius = 6.0
weight_unit = 0.25
f32 = jnp.float32
bf16 = jnp.bfloat16


def dot(a, b):
    return jnp.dot(a, b, preferred_element_type=f32)


def col_dft(npix):
    half = npix // 2
    product = np.arange(npix)[:, None] * np.arange(half)[None, :] % npix
    phases = product.astype(np.float32) * np.float32(2.0 * math.pi / npix)
    factor = np.float32(1.0 / math.sqrt(npix))
    table = np.concatenate([np.cos(phases) * factor, -np.sin(phases) * factor], axis=1)
    return jnp.asarray(table.astype(jnp.bfloat16))


def side_cols(k, width):
    return jnp.where(k < MARGIN, k - MARGIN, width - MARGIN + k)


def toeplitz(taps, index):
    out = jnp.zeros((NB,) + index.shape, f32)
    for t in range(TAPS):
        out = jnp.where(index[None] == t, taps[:, t][:, None, None], out)
    return out


def adjoint_tables(row_taps, col_taps, width, block):
    h = row_taps.astype(bf16).astype(f32)
    g = col_taps.astype(bf16).astype(f32)
    i = jnp.arange(width)[:, None]
    j = jnp.arange(width)[None, :]
    main = toeplitz(g, j - i + MARGIN)
    k = jnp.arange(width)[None, :]
    side_index = jnp.where(k < 2 * MARGIN, side_cols(k, width) - i + MARGIN, -1)
    side = toeplitz(g, side_index)
    cols = jnp.concatenate([main, side], axis=2).astype(bf16)
    r = jnp.arange(block)[:, None]
    w = jnp.arange(NB * (block + 2 * PAD))[None, :]
    span = block + 2 * PAD
    rows = jnp.zeros((block, NB * span), f32)
    index = r - w % span + PAD + MARGIN
    for t in range(TAPS):
        tap_row = jnp.repeat(h[:, t], span)[None, :]
        rows = jnp.where(index == t, tap_row, rows)
    return cols, rows.astype(bf16)


def forward_tables(row_taps, col_taps, width, block):
    h = row_taps.astype(bf16).astype(f32)
    g = col_taps.astype(bf16).astype(f32)
    i = jnp.arange(width)[:, None]
    j = jnp.arange(NB * width)[None, :]
    main_index = i - j % width + MARGIN
    side_index = jnp.where(i < 2 * MARGIN, side_cols(i, width) - j % width + MARGIN, -1)
    index = jnp.concatenate([main_index, side_index], axis=0)
    cols = jnp.zeros(index.shape, f32)
    for t in range(TAPS):
        tap_row = jnp.repeat(g[:, t], width)[None, :]
        cols = jnp.where(index == t, tap_row, cols)
    r = jnp.arange(block)[:, None]
    w = jnp.arange(block + 2 * PAD)[None, :]
    rows = toeplitz(h, w - r - PAD + MARGIN)
    return cols.astype(bf16), rows.astype(bf16)


def spill_tables(fcols, width):
    span = 2 * MARGIN
    row = jnp.arange(fcols * span)[:, None]
    col = jnp.arange(fcols * width)[None, :]
    rb, rk = row // span, row % span
    gather = jnp.where(rk >= MARGIN, (rb + 1) * width + rk - MARGIN, rb * width - MARGIN + rk)
    table = (gather == col).astype(bf16)
    return table


def adjoint_group(R, W, B, first, channel, u, up, lo, gcols, hrows, adj, adjs, dc, dcs, main_done, side_done):
    per = W // 16
    span = B + 2 * PAD
    mains = [gcols[n, :, :W] for n in range(NB)]
    hr = hrows[...]
    for pair in range(0, per, 2):
        for n in range(NB):
            acc = None
            for e in range(2):
                c = channel(first + pair + e)
                shift = 16 * (pair + e)
                side = gcols[n, :, W:].astype(f32)
                side = pltpu.roll(side, shift, 1) if shift else side
                table = jnp.concatenate([mains[n], side.astype(bf16)], axis=1)
                rows = jnp.concatenate([up[n, c], u[n, c], lo[n, c]], axis=0)
                out = dot(rows, table)
                dc[n, :, e * W : (e + 1) * W] = out[:, :W].astype(bf16)
                acc = out[:, W:] if acc is None else acc + out[:, W:]
            if pair:
                dcs[n] = dcs[n] + acc.astype(bf16)
            else:
                dcs[n] = acc.astype(bf16)
        for k in range(R // B):
            win = jnp.concatenate([dc[n, k * B : k * B + span] for n in range(NB)], axis=0)
            out = dot(hr, win).astype(bf16)
            adj[first + pair, k * B : k * B + B] = out[:, :W]
            adj[first + pair + 1, k * B : k * B + B] = out[:, W:]
        main_done(first + pair)
        main_done(first + pair + 1)
    for k in range(R // B):
        win = jnp.concatenate([dcs[n, k * B : k * B + span] for n in range(NB)], axis=0)
        out = dot(hr, win).T.astype(bf16)
        for cc in range(per):
            adjs[first + cc, :, k * B : k * B + B] = out[cc * 16 : cc * 16 + 16]
    for cc in range(per):
        side_done(first + cc)


def half_body(FC, W, x, colT, out):
    full = out.shape[1]
    rows = jnp.concatenate([x[b] for b in range(FC)], axis=1)

    @pl.loop(0, full // 256)
    def _(j):
        lanes = pl.ds(pl.multiple_of(j * 256, 256), 256)
        out[:, lanes] = dot(rows, colT[:, lanes]).astype(bf16)


def table_body(s, FR, R, colT, bown, aown, aoth):
    half = FR * R
    for a in range(FR):
        own = pl.ds(pl.multiple_of((2 * a + s) * R, R), R)
        bown[a * R : (a + 1) * R] = colT[own, :]
    sign_row = lax.broadcasted_iota(jnp.int32, (1, half), 1) % 2
    flip = jnp.where((sign_row == 1) & (s == 1), -1.0, 1.0).astype(f32)
    for dst, part in ((aown, s), (aoth, 1 - s)):
        for q in range(2):
            pieces = [
                colT[pl.ds(pl.multiple_of((2 * a + part) * R, R), R), q * half : (q + 1) * half]
                for a in range(FR)
            ]
            block = jnp.concatenate(pieces, axis=0) if FR > 1 else pieces[0]
            dst[:, q * half : (q + 1) * half] = (block.astype(f32).T * flip).astype(bf16)


def stack_re_im(ref, lanes_re, lanes_im, transpose):
    re, im = ref[:, lanes_re], ref[:, lanes_im]
    if transpose:
        return jnp.concatenate([re, im], 0), jnp.concatenate([im, -re], 0)
    return jnp.concatenate([re, -im], 0), jnp.concatenate([im, re], 0)


def vis_body(half, aown, aoth, hown, hoth, wts, out):
    step = 256

    @pl.loop(0, half // step)
    def _(j):
        re_l = pl.ds(pl.multiple_of(j * step, step), step)
        im_l = pl.ds(pl.multiple_of(j * step + half, step), step)
        own_re, own_im = stack_re_im(hown, re_l, im_l, False)
        oth_re, oth_im = stack_re_im(hoth, re_l, im_l, False)
        scale = weight_unit * wts[:, re_l].astype(f32)
        re = dot(aown[...], own_re) + dot(aoth[...], oth_re)
        out[:, re_l] = (scale * re).astype(bf16)
        im = dot(aown[...], own_im) + dot(aoth[...], oth_im)
        out[:, im_l] = (scale * im).astype(bf16)


def back_body(s, half, bown, wown, woth, out):
    step = 256
    odd = lax.broadcasted_iota(jnp.int32, (half, 1), 0) % 2 == 1
    own_sign = jnp.where(odd & (s == 1), -1.0, 1.0)
    oth_sign = jnp.where(odd & (s == 0), -1.0, 1.0)

    @pl.loop(0, half // step)
    def _(j):
        re_l = pl.ds(pl.multiple_of(j * step, step), step)
        im_l = pl.ds(pl.multiple_of(j * step + half, step), step)
        own_re, own_im = stack_re_im(wown, re_l, im_l, True)
        oth_re, oth_im = stack_re_im(woth, re_l, im_l, True)
        re = own_sign * dot(bown[...], own_re) + oth_sign * dot(bown[...], oth_re)
        out[:, re_l] = re.astype(bf16)
        im = own_sign * dot(bown[...], own_im) + oth_sign * dot(bown[...], oth_im)
        out[:, im_l] = im.astype(bf16)


def gradient_body(FC, W, back, colT, x, d, pre):
    step = 2 * W

    @pl.loop(0, FC // 2)
    def _(j):
        lanes = pl.ds(pl.multiple_of(j * step, step), step)
        grad = lax.dot_general(
            back[...], colT[lanes, :], (((1,), (1,)), ((), ())), preferred_element_type=f32
        )
        xs = jnp.concatenate([x[2 * j], x[2 * j + 1]], axis=1).astype(f32)
        ds = jnp.concatenate([d[2 * j], d[2 * j + 1]], axis=1).astype(f32)
        pre[:, lanes] = xs - primal_step * (grad - ds)


def side_rows(FC, FR, adjs):
    st_rows = []
    for a in range(FR):
        parts = jnp.concatenate([adjs[b * FR + a] for b in range(FC)], axis=0)
        st_rows.append(parts.astype(f32).T.astype(bf16))
    return jnp.concatenate(st_rows, axis=0) if FR > 1 else st_rows[0]


def forward_cols_body(C, R, W, main, sides, fcols, ic):
    per = W // 16
    for c0 in range(0, C, per):
        parts = jnp.concatenate([sides[c0 + cc] for cc in range(per)], axis=0)
        st = parts.astype(f32).T.astype(bf16)
        for cc in range(per):
            c = c0 + cc
            zeros_a = jnp.zeros((cc * 16, NB * W), bf16)
            zeros_b = jnp.zeros((W - 16 - cc * 16, NB * W), bf16)
            pieces = [fcols[:W], fcols[W : W + 16]]
            if cc:
                pieces.insert(1, zeros_a)
            if cc < per - 1:
                pieces.append(zeros_b)
            table = jnp.concatenate(pieces, axis=0)
            out = dot(jnp.concatenate([main[c], st], axis=1), table)
            for n in range(NB):
                ic[n, PAD : PAD + R, c * W : (c + 1) * W] = out[:, n * W : (n + 1) * W].astype(bf16)


def shrink_body(C, R, W, B, ic, frows, u, mask, new_in, out, new_out):
    span = B + 2 * PAD
    new_out[...] = new_in[...]
    hr = frows[0]
    for k in range(R // B):
        rows = slice(k * B, (k + 1) * B)
        keep = radius * mask[rows].astype(f32)
        coef = dot(hr, ic[0, k * B : k * B + span])
        total = None
        steps = []
        for c in range(C):
            st = u[0, c, rows].astype(f32) + dual_step * coef[:, c * W : (c + 1) * W]
            steps.append(st)
            total = st * st if total is None else total + st * st
        scale = keep / jnp.maximum(jnp.sqrt(total), radius)
        for c in range(C):
            out[0, c, rows] = (steps[c] * scale).astype(bf16)


def step_kernel(
    C, FC, FR, R, W, B,
    u, x, d, wts, colT, spill, gcols, hrows, fcols,
    new, ic,
    up, lo, dc, dcs, adj, adjs, radj, radjs,
    hown, hoth, wown, woth, back, bown, aown, aoth, pre,
    ext, exts, rmain, rsides, htop, hbot,
    send_u, recv_u, send_a, recv_a, send_as, recv_as,
    send_e, recv_e, send_es, recv_es, send_p, recv_p, send_h, recv_h,
):
    half = FC * W // 2
    me = lax.axis_index("chan")
    s = lax.axis_index("split")
    ma, mb = me % FR, me // FR
    has_up = (ma > 0) | (s == 1)
    has_down = (ma < FR - 1) | (s == 0)
    partner = {"chan": me, "split": 1 - s}
    down_id = {"chan": (me + s) % C, "split": 1 - s}
    up_id = {"chan": (me + s + C - 1) % C, "split": 1 - s}
    per = W // 16

    def remote(src, dst, ssem, rsem, device):
        return pltpu.make_async_remote_copy(
            src_ref=src, dst_ref=dst, send_sem=ssem, recv_sem=rsem,
            device_id=device, device_id_type=pl.DeviceIdType.MESH,
        )

    barrier = pltpu.get_barrier_semaphore()

    @pl.loop(1, C)
    def _(i):
        pl.semaphore_signal(
            barrier, inc=1, device_id={"chan": (me + i) % C, "split": s},
            device_id_type=pl.DeviceIdType.MESH,
        )

    pl.semaphore_signal(barrier, inc=1, device_id=partner, device_id_type=pl.DeviceIdType.MESH)
    if FR > 1:
        cross = jnp.where(s == 0, ma > 0, ma < FR - 1)
        cross_chan = jnp.where(s == 0, (me + C - 1) % C, (me + 1) % C)

        @pl.when(cross)
        def _():
            pl.semaphore_signal(
                barrier, inc=1, device_id={"chan": cross_chan, "split": 1 - s},
                device_id_type=pl.DeviceIdType.MESH,
            )
            pl.semaphore_wait(barrier, 1)

    pl.semaphore_wait(barrier, C)

    def chain(down_src, down_dst, up_src, up_dst, ssem, rsem):
        downward = remote(down_src, down_dst, ssem.at[0], rsem.at[0], down_id)
        upward = remote(up_src, up_dst, ssem.at[1], rsem.at[1], up_id)

        @pl.when(has_down)
        def _():
            downward.start()

        @pl.when(has_up)
        def _():
            upward.start()

        @pl.when(jnp.logical_not(has_up))
        def _():
            down_dst[...] = jnp.zeros_like(down_dst)

        @pl.when(jnp.logical_not(has_down))
        def _():
            up_dst[...] = jnp.zeros_like(up_dst)

        def finish():
            @pl.when(has_down)
            def _():
                downward.wait_send()
                upward.wait_recv()

            @pl.when(has_up)
            def _():
                upward.wait_send()
                downward.wait_recv()

        return finish

    finish_u = chain(u.at[:, :, pl.ds(R - PAD, PAD)], up, u.at[:, :, pl.ds(0, PAD)], lo, send_u, recv_u)
    table_body(s, FR, R, colT, bown, aown, aoth)
    finish_u()

    def peer(i):
        return (me + 1 + i) % C

    def send(buf, dst, ssem, rsem):
        def start(i):
            @pl.when(i < C - 1)
            def _():
                remote(
                    buf.at[i], dst.at[me], ssem.at[i], rsem.at[i], {"chan": peer(i), "split": s}
                ).start()

            @pl.when(i == C - 1)
            def _():
                dst[me] = buf[i]

        return start

    def finish(buf, dst, ssem, rsem):
        @pl.loop(0, C - 1)
        def _(i):
            remote(
                buf.at[i], dst.at[me], ssem.at[i], rsem.at[i], {"chan": peer(i), "split": s}
            ).wait()

    @pl.loop(0, C // per)
    def _(g):
        adjoint_group(
            R, W, B, g * per, peer, u, up, lo, gcols, hrows, adj, adjs, dc, dcs,
            send(adj, radj, send_a, recv_a), send(adjs, radjs, send_as, recv_as),
        )

    half_body(FC, W, x, colT, hown)
    copy = remote(hown, hoth, send_p.at[0], recv_p.at[0], partner)
    copy.start()
    copy.wait()
    vis_body(half, aown, aoth, hown, hoth, wts, wown)
    copy = remote(wown, woth, send_p.at[1], recv_p.at[1], partner)
    copy.start()
    copy.wait()
    back_body(s, half, bown, wown, woth, back)
    gradient_body(FC, W, back, colT, x, d, pre)

    finish(adjs, radjs, send_as, recv_as)
    finish(adj, radj, send_a, recv_a)
    st = side_rows(FC, FR, radjs)
    es = None
    for i in range(FC):
        b = (mb + 1 + i) % FC
        lanes = pl.ds(pl.multiple_of(b * W, W), W)
        table = spill[:, lanes]
        pieces = [radj[b * FR + a] for a in range(FR)]
        main = jnp.concatenate(pieces, axis=0) if FR > 1 else pieces[0]
        upd = pre[:, lanes] - primal_step * (main.astype(f32) + dot(st, table))
        nb = jnp.maximum(upd, 0.0).astype(bf16)
        eb = (2.0 * nb.astype(f32) - x[b].astype(f32)).astype(bf16)
        new[b] = nb
        for a in range(FR):
            ext[b * FR + a] = eb[a * R : (a + 1) * R]
        part = lax.dot_general(eb, table, (((1,), (1,)), ((), ())), preferred_element_type=f32)
        es = part if es is None else es + part
        for j in range(FR):
            f = b * FR + (ma + j) % FR
            r = i * FR + j
            if i == FC - 1 and j == 0:
                rmain[me] = eb if FR == 1 else ext[f]
            else:
                remote(
                    ext.at[f], rmain.at[me], send_e.at[r], recv_e.at[r], {"chan": f, "split": s}
                ).start()
    for a in range(FR):
        t = es[a * R : (a + 1) * R].T.astype(bf16)
        for b in range(FC):
            exts[b * FR + a] = t[b * 16 : b * 16 + 16]
    sides = []
    for i in range(FC):
        for j in range(FR):
            f = (mb + 1 + i) % FC * FR + (ma + j) % FR
            r = i * FR + j
            if i == FC - 1 and j == 0:
                rsides[me] = exts[f]
            else:
                remote(
                    exts.at[f], rsides.at[me], send_es.at[r], recv_es.at[r],
                    {"chan": f, "split": s},
                ).start()
    for i in range(FC):
        for j in range(FR):
            f = (mb + 1 + i) % FC * FR + (ma + j) % FR
            r = i * FR + j
            if i == FC - 1 and j == 0:
                continue
            device = {"chan": f, "split": s}
            remote(exts.at[f], rsides.at[me], send_es.at[r], recv_es.at[r], device).wait()
            remote(ext.at[f], rmain.at[me], send_e.at[r], recv_e.at[r], device).wait()
    forward_cols_body(C, R, W, rmain, rsides, fcols, ic)
    finish_h = chain(
        ic.at[:, pl.ds(R, PAD)], htop, ic.at[:, pl.ds(PAD, PAD)], hbot, send_h, recv_h
    )
    finish_h()
    ic[:, :PAD] = htop[...]
    ic[:, PAD + R :] = hbot[...]


def per_device(sky_image, dirty_image, uv_weights, dual_coeffs, support_mask, row_taps, col_taps):
    FC, FR = sky_image.shape[1], sky_image.shape[2]
    R, W = sky_image.shape[4], sky_image.shape[5]
    C = dual_coeffs.shape[1]
    npix = FC * W
    half = npix // 2
    B = min(128, R)
    RP = R + 2 * PAD
    u = dual_coeffs.reshape(NB, C, R, W)
    x = sky_image.reshape(FC, FR * R, W)
    d = dirty_image.reshape(FC, FR * R, W)
    wts = uv_weights.reshape(half, half)
    mask = support_mask.reshape(R, W)
    colT = col_dft(npix)
    spill = spill_tables(FC, W)
    gcols, hrows = adjoint_tables(row_taps, col_taps, W, B)
    fcols, frows = forward_tables(row_taps, col_taps, W, B)
    vm = lambda *shape: pltpu.VMEM(shape, bf16)
    sem = lambda n: pltpu.SemaphoreType.DMA((n,))
    new, ic = pl.pallas_call(
        functools.partial(step_kernel, C, FC, FR, R, W, B),
        out_shape=[
            jax.ShapeDtypeStruct((FC, FR * R, W), bf16),
            jax.ShapeDtypeStruct((NB, RP, C * W), bf16),
        ],
        scratch_shapes=[
            vm(NB, C, PAD, W), vm(NB, C, PAD, W), vm(NB, RP, 2 * W), vm(NB, RP, W),
            vm(C, R, W), vm(C, 16, R), vm(C, R, W), vm(C, 16, R),
            *[vm(half, npix)] * 8, pltpu.VMEM((half, npix), f32),
            vm(C, R, W), vm(C, 16, R), vm(C, R, W), vm(C, 16, R),
            vm(NB, PAD, C * W), vm(NB, PAD, C * W),
            sem(2), sem(2), sem(C), sem(C), sem(C), sem(C),
            sem(C), sem(C), sem(C), sem(C), sem(2), sem(2), sem(2), sem(2),
        ],
        compiler_params=pltpu.CompilerParams(
            collective_id=0, has_side_effects=True, vmem_limit_bytes=58 * 2**20
        ),
    )(u, x, d, wts, colT, spill, gcols, hrows, fcols)

    part = FC // NB
    new_dual, new = pl.pallas_call(
        functools.partial(shrink_body, C, R, W, B),
        grid=(NB,),
        in_specs=[
            pl.BlockSpec((1, RP, C * W), lambda n: (n, 0, 0)),
            pl.BlockSpec((1, B, B + 2 * PAD), lambda n: (n, 0, 0)),
            pl.BlockSpec((1, C, R, W), lambda n: (n, 0, 0, 0)),
            pl.BlockSpec((R, W), lambda n: (0, 0)),
            pl.BlockSpec((part, FR * R, W), lambda n: (n, 0, 0)),
        ],
        out_specs=[
            pl.BlockSpec((1, C, R, W), lambda n: (n, 0, 0, 0)),
            pl.BlockSpec((part, FR * R, W), lambda n: (n, 0, 0)),
        ],
        out_shape=[
            jax.ShapeDtypeStruct((NB, C, R, W), bf16),
            jax.ShapeDtypeStruct((FC, FR * R, W), bf16),
        ],
    )(ic, frows, u, mask, new)
    return (new.reshape(sky_image.shape), new_dual.reshape(dual_coeffs.shape))


def solution(mesh):
    placed = (
        P(("cube", "chan"), None, None, "split", None, None),
        P(("cube", "chan"), None, None, "split", None, None),
        P(("cube", "chan"), "split", None),
        P(None, "cube", "chan", "split", None, None),
        P("chan", "split", None, None),
        P(),
        P(),
    )
    return jax.shard_map(
        per_device,
        mesh=mesh,
        in_specs=placed,
        out_specs=(
            P(("cube", "chan"), None, None, "split", None, None),
            P(None, "cube", "chan", "split", None, None),
        ),
        check_vma=False,
    )
```

```python
import functools
import math

import jax
import jax.numpy as jnp
import numpy as np
from jax import lax
from jax.experimental import pallas as pl
from jax.experimental.pallas import tpu as pltpu
from jax.sharding import PartitionSpec as P

NB = 4
TAPS = 17
MARGIN = 8
PAD = 16

primal_step = 0.5
dual_step = 0.5
radius = 6.0
weight_unit = 0.25
f32 = jnp.float32
bf16 = jnp.bfloat16


def dot(a, b):
    return jnp.dot(a, b, preferred_element_type=f32)


def col_dft(npix):
    half = npix // 2
    product = np.arange(npix)[:, None] * np.arange(half)[None, :] % npix
    phases = product.astype(np.float32) * np.float32(2.0 * math.pi / npix)
    factor = np.float32(1.0 / math.sqrt(npix))
    table = np.concatenate([np.cos(phases) * factor, -np.sin(phases) * factor], axis=1)
    return jnp.asarray(table.astype(jnp.bfloat16))


def bands(index, taps):
    outs = [jnp.zeros(index.shape, f32) for _ in range(NB)]
    for t in range(TAPS):
        hit = index == t
        outs = [jnp.where(hit, taps[n, t], outs[n]) for n in range(NB)]
    return [o.astype(bf16) for o in outs]


def adjoint_tables(W, B, row_taps, col_taps, gcols, hrows):
    i = lax.broadcasted_iota(jnp.int32, (W, W), 0)
    j = lax.broadcasted_iota(jnp.int32, (W, W), 1)
    side = jnp.where(j < MARGIN, j - MARGIN, W - MARGIN + j)
    main_bands = bands(j - i + MARGIN, col_taps)
    side_bands = bands(jnp.where(j < 2 * MARGIN, side - i + MARGIN, -1), col_taps)
    r = lax.broadcasted_iota(jnp.int32, (B, B + 2 * PAD), 0)
    w = lax.broadcasted_iota(jnp.int32, (B, B + 2 * PAD), 1)
    row_bands = bands(r - w + PAD + MARGIN, row_taps)
    for n in range(NB):
        gcols[n, :, :W] = main_bands[n]
        gcols[n, :, W:] = side_bands[n]
        hrows[n] = row_bands[n]


def forward_tables(W, B, row_taps, col_taps, fcols, frows):
    i = lax.broadcasted_iota(jnp.int32, (W, W), 0)
    j = lax.broadcasted_iota(jnp.int32, (W, W), 1)
    main_bands = bands(i - j + MARGIN, col_taps)
    k = lax.broadcasted_iota(jnp.int32, (2 * MARGIN, W), 0)
    jk = lax.broadcasted_iota(jnp.int32, (2 * MARGIN, W), 1)
    side = jnp.where(k < MARGIN, k - MARGIN, W - MARGIN + k)
    side_bands = bands(side - jk + MARGIN, col_taps)
    r = lax.broadcasted_iota(jnp.int32, (B, B + 2 * PAD), 0)
    w = lax.broadcasted_iota(jnp.int32, (B, B + 2 * PAD), 1)
    row_bands = bands(w - r - PAD + MARGIN, row_taps)
    for n in range(NB):
        fcols[:W, n * W : (n + 1) * W] = main_bands[n]
        fcols[W:, n * W : (n + 1) * W] = side_bands[n]
        frows[n] = row_bands[n]


def spill_table(FC, W, spill):
    span = 2 * MARGIN
    row = lax.broadcasted_iota(jnp.int32, (FC * span, FC * W), 0)
    col = lax.broadcasted_iota(jnp.int32, (FC * span, FC * W), 1)
    rb, rk = row // span, row % span
    target = jnp.where(rk >= MARGIN, (rb + 1) * W + rk - MARGIN, rb * W - MARGIN + rk)
    spill[...] = jnp.where(target == col, 1.0, 0.0).astype(bf16)


def adjoint_group(R, W, B, first, channel, u, up, lo, gcols, hrows, adj, adjs, dc, dcs, main_done, side_done):
    per = W // 16
    span = B + 2 * PAD
    mains = [gcols[n, :, :W] for n in range(NB)]
    for pair in range(0, per, 2):
        for n in range(NB):
            acc = None
            for e in range(2):
                c = channel(first + pair + e)
                shift = 16 * (pair + e)
                side = gcols[n, :, W:].astype(f32)
                side = pltpu.roll(side, shift, 1) if shift else side
                table = jnp.concatenate([mains[n], side.astype(bf16)], axis=1)
                rows = jnp.concatenate([up[n, c], u[n, c], lo[n, c]], axis=0)
                out = dot(rows, table)
                dc[n, :, e * W : (e + 1) * W] = out[:, :W].astype(bf16)
                acc = out[:, W:] if acc is None else acc + out[:, W:]
            if pair:
                dcs[n] = dcs[n] + acc.astype(bf16)
            else:
                dcs[n] = acc.astype(bf16)
        for k in range(R // B):
            out = sum(dot(hrows[n], dc[n, k * B : k * B + span]) for n in range(NB)).astype(bf16)
            adj[first + pair, k * B : k * B + B] = out[:, :W]
            adj[first + pair + 1, k * B : k * B + B] = out[:, W:]
        main_done(first + pair)
        main_done(first + pair + 1)
    for k in range(R // B):
        out = sum(dot(hrows[n], dcs[n, k * B : k * B + span]) for n in range(NB)).T.astype(bf16)
        for cc in range(per):
            adjs[first + cc, :, k * B : k * B + B] = out[cc * 16 : cc * 16 + 16]
    for cc in range(per):
        side_done(first + cc)


def half_chunk(FC, x, colT, out, lanes):
    rows = jnp.concatenate([x[b] for b in range(FC)], axis=1)
    out[:, lanes] = dot(rows, colT[:, lanes]).astype(bf16)


def table_body(s, FR, R, colT, bown, aown, aoth):
    half = FR * R
    for a in range(FR):
        own = pl.ds(pl.multiple_of((2 * a + s) * R, R), R)
        bown[a * R : (a + 1) * R] = colT[own, :]
    odd_lane = lax.broadcasted_iota(jnp.int32, (1, half), 1) % 2 == 1
    flip = jnp.where(odd_lane & (s == 1), -1.0, 1.0).astype(f32)
    odd_row = lax.broadcasted_iota(jnp.int32, (half, 1), 0) % 2 == 1
    for dst, part in ((aown, s), (aoth, 1 - s)):
        for q in range(2):
            lanes = slice(q * half, (q + 1) * half)
            if FR == 1:
                sign = jnp.where(odd_row & (part == 1), -1.0, 1.0).astype(f32)
                dst[:, lanes] = (colT[:half, lanes].astype(f32) * (sign * flip)).astype(bf16)
                continue
            pieces = [
                colT[pl.ds(pl.multiple_of((2 * a + part) * R, R), R), lanes] for a in range(FR)
            ]
            block = jnp.concatenate(pieces, axis=0)
            dst[:, lanes] = (block.astype(f32).T * flip).astype(bf16)


def stack_re_im(ref, lanes_re, lanes_im, transpose):
    re, im = ref[:, lanes_re], ref[:, lanes_im]
    if transpose:
        return jnp.concatenate([re, im], 0), jnp.concatenate([im, -re], 0)
    return jnp.concatenate([re, -im], 0), jnp.concatenate([im, re], 0)


def vis_chunk(aown, aoth, hown, hoth, wts, out, re_l, im_l):
    own_re, own_im = stack_re_im(hown, re_l, im_l, False)
    oth_re, oth_im = stack_re_im(hoth, re_l, im_l, False)
    scale = weight_unit * wts[:, re_l].astype(f32)
    re = dot(aown[...], own_re) + dot(aoth[...], oth_re)
    out[:, re_l] = (scale * re).astype(bf16)
    im = dot(aown[...], own_im) + dot(aoth[...], oth_im)
    out[:, im_l] = (scale * im).astype(bf16)


def back_chunk(s, half, bown, wown, woth, out, re_l, im_l):
    odd = lax.broadcasted_iota(jnp.int32, (half, 1), 0) % 2 == 1
    own_sign = jnp.where(odd & (s == 1), -1.0, 1.0)
    oth_sign = jnp.where(odd & (s == 0), -1.0, 1.0)
    own_re, own_im = stack_re_im(wown, re_l, im_l, True)
    oth_re, oth_im = stack_re_im(woth, re_l, im_l, True)
    re = own_sign * dot(bown[...], own_re) + oth_sign * dot(bown[...], oth_re)
    out[:, re_l] = re.astype(bf16)
    im = own_sign * dot(bown[...], own_im) + oth_sign * dot(bown[...], oth_im)
    out[:, im_l] = im.astype(bf16)


def gradient_body(FC, W, back, colT, x, d, pre):
    step = 2 * W

    @pl.loop(0, FC // 2)
    def _(j):
        lanes = pl.ds(pl.multiple_of(j * step, step), step)
        grad = lax.dot_general(
            back[...], colT[lanes, :], (((1,), (1,)), ((), ())), preferred_element_type=f32
        )
        xs = jnp.concatenate([x[2 * j], x[2 * j + 1]], axis=1).astype(f32)
        ds = jnp.concatenate([d[2 * j], d[2 * j + 1]], axis=1).astype(f32)
        pre[:, lanes] = xs - primal_step * (grad - ds)


def side_rows(FC, FR, adjs):
    st_rows = []
    for a in range(FR):
        parts = jnp.concatenate([adjs[b * FR + a] for b in range(FC)], axis=0)
        st_rows.append(parts.astype(f32).T.astype(bf16))
    return jnp.concatenate(st_rows, axis=0) if FR > 1 else st_rows[0]


def forward_cols(R, W, c, main, sides, fcols, ic):
    out = dot(main[c], fcols[:W]) + lax.dot_general(
        sides[c], fcols[W:], (((0,), (0,)), ((), ())), preferred_element_type=f32
    )
    lanes = pl.ds(pl.multiple_of(c * W, W), W)
    for n in range(NB):
        ic[n, PAD : PAD + R, lanes] = out[:, n * W : (n + 1) * W].astype(bf16)


def shrink_body(C, R, W, B, ic, frows, u, mask, new_in, out, new_out):
    span = B + 2 * PAD
    new_out[...] = new_in[...]
    hr = frows[0]
    for k in range(R // B):
        rows = slice(k * B, (k + 1) * B)
        keep = radius * mask[rows].astype(f32)
        coef = dot(hr, ic[0, k * B : k * B + span])
        total = None
        steps = []
        for c in range(C):
            st = u[0, c, rows].astype(f32) + dual_step * coef[:, c * W : (c + 1) * W]
            steps.append(st)
            total = st * st if total is None else total + st * st
        scale = keep / jnp.maximum(jnp.sqrt(total), radius)
        for c in range(C):
            out[0, c, rows] = (steps[c] * scale).astype(bf16)


def step_kernel(
    C, FC, FR, R, W, B,
    u_hbm, x_hbm, d_hbm, wts_hbm, colT_hbm, row_taps, col_taps,
    new, ic, frows,
    u, x, d, wts, colT, spill, gcols, hrows, fcols,
    up, lo, dc, dcs, adj, adjs, radj, radjs,
    hown, hoth, wown, woth, back, bown, aown, aoth, pre,
    ext, exts, rmain, rsides, htop, hbot,
    send_u, recv_u, send_a, recv_a, send_as, recv_as,
    send_e, recv_e, send_es, recv_es, send_p, recv_p, send_h, recv_h, load,
):
    half = FC * W // 2
    me = lax.axis_index("chan")
    s = lax.axis_index("split")
    ma, mb = me % FR, me // FR
    has_up = (ma > 0) | (s == 1)
    has_down = (ma < FR - 1) | (s == 0)
    partner = {"chan": me, "split": 1 - s}
    down_id = {"chan": (me + s) % C, "split": 1 - s}
    up_id = {"chan": (me + s + C - 1) % C, "split": 1 - s}
    per = W // 16

    def remote(src, dst, ssem, rsem, device):
        return pltpu.make_async_remote_copy(
            src_ref=src, dst_ref=dst, send_sem=ssem, recv_sem=rsem,
            device_id=device, device_id_type=pl.DeviceIdType.MESH,
        )

    loads = [
        pltpu.make_async_copy(a, b, load.at[i])
        for i, (a, b) in enumerate(
            [(u_hbm, u), (colT_hbm, colT), (x_hbm, x), (wts_hbm, wts), (d_hbm, d)]
        )
    ]
    for copy in loads:
        copy.start()
    barrier = pltpu.get_barrier_semaphore()

    @pl.loop(1, C)
    def _(i):
        pl.semaphore_signal(
            barrier, inc=1, device_id={"chan": (me + i) % C, "split": s},
            device_id_type=pl.DeviceIdType.MESH,
        )

    pl.semaphore_signal(barrier, inc=1, device_id=partner, device_id_type=pl.DeviceIdType.MESH)
    if FR > 1:
        cross = jnp.where(s == 0, ma > 0, ma < FR - 1)
        cross_chan = jnp.where(s == 0, (me + C - 1) % C, (me + 1) % C)

        @pl.when(cross)
        def _():
            pl.semaphore_signal(
                barrier, inc=1, device_id={"chan": cross_chan, "split": 1 - s},
                device_id_type=pl.DeviceIdType.MESH,
            )
            pl.semaphore_wait(barrier, 1)

    adjoint_tables(W, B, row_taps, col_taps, gcols, hrows)
    loads[0].wait()
    pl.semaphore_wait(barrier, C)

    def chain(down_src, down_dst, up_src, up_dst, ssem, rsem):
        downward = remote(down_src, down_dst, ssem.at[0], rsem.at[0], down_id)
        upward = remote(up_src, up_dst, ssem.at[1], rsem.at[1], up_id)

        @pl.when(has_down)
        def _():
            downward.start()

        @pl.when(has_up)
        def _():
            upward.start()

        @pl.when(jnp.logical_not(has_up))
        def _():
            down_dst[...] = jnp.zeros_like(down_dst)

        @pl.when(jnp.logical_not(has_down))
        def _():
            up_dst[...] = jnp.zeros_like(up_dst)

        def finish():
            @pl.when(has_down)
            def _():
                downward.wait_send()
                upward.wait_recv()

            @pl.when(has_up)
            def _():
                upward.wait_send()
                downward.wait_recv()

        return finish

    finish_u = chain(u.at[:, :, pl.ds(R - PAD, PAD)], up, u.at[:, :, pl.ds(0, PAD)], lo, send_u, recv_u)
    loads[1].wait()
    table_body(s, FR, R, colT, bown, aown, aoth)
    finish_u()

    def peer(i):
        return (me + 1 + i) % C

    def send(buf, dst, ssem, rsem):
        def start(i):
            @pl.when(i < C - 1)
            def _():
                remote(
                    buf.at[i], dst.at[me], ssem.at[i], rsem.at[i], {"chan": peer(i), "split": s}
                ).start()

            @pl.when(i == C - 1)
            def _():
                dst[me] = buf[i]

        return start

    def finish(buf, dst, ssem, rsem):
        @pl.loop(0, C - 1)
        def _(i):
            remote(
                buf.at[i], dst.at[me], ssem.at[i], rsem.at[i], {"chan": peer(i), "split": s}
            ).wait()

    @pl.loop(0, C // per)
    def _(g):
        adjoint_group(
            R, W, B, g * per, peer, u, up, lo, gcols, hrows, adj, adjs, dc, dcs,
            send(adj, radj, send_a, recv_a), send(adjs, radjs, send_as, recv_as),
        )

    for copy in loads[2:]:
        copy.wait()
    step = 256
    chunks = half // step

    def to_partner(buf, dst, lanes, i):
        return remote(buf.at[:, lanes], dst.at[:, lanes], send_p.at[i], recv_p.at[i], partner)

    def parts(j):
        return pl.ds(j * step, step), pl.ds(half + j * step, step)

    copies = []
    for j in range(chunks):
        for q, lanes in enumerate(parts(j)):
            half_chunk(FC, x, colT, hown, lanes)
            copy = to_partner(hown, hoth, lanes, 2 * j + q)
            copy.start()
            copies.append(copy)
    spill_table(FC, W, spill)
    second = []
    for j in range(chunks):
        copies[2 * j].wait()
        copies[2 * j + 1].wait()
        vis_chunk(aown, aoth, hown, hoth, wts, wown, *parts(j))
        for q, lanes in enumerate(parts(j)):
            copy = to_partner(wown, woth, lanes, 2 * chunks + 2 * j + q)
            copy.start()
            second.append(copy)
    for j in range(chunks):
        second[2 * j].wait()
        second[2 * j + 1].wait()
        back_chunk(s, half, bown, wown, woth, back, *parts(j))
    gradient_body(FC, W, back, colT, x, d, pre)

    finish(adjs, radjs, send_as, recv_as)
    finish(adj, radj, send_a, recv_a)
    st = side_rows(FC, FR, radjs)
    k = lax.broadcasted_iota(jnp.int32, (2 * MARGIN, W), 0)
    col = lax.broadcasted_iota(jnp.int32, (2 * MARGIN, W), 1)
    take_left = jnp.where((k < MARGIN) & (col == W - MARGIN + k), 1.0, 0.0)
    take_right = jnp.where((k >= MARGIN) & (col == k - MARGIN), 1.0, 0.0)

    def deliver(buf, dst, ssem, rsem, i, start):
        b = (mb + i) % FC
        for j in range(FR):
            f = b * FR + (ma + j) % FR
            r = i * FR + j
            if r == 0:
                if start:
                    dst[me] = buf[f]
                continue
            copy = remote(buf.at[f], dst.at[me], ssem.at[r], rsem.at[r], {"chan": f, "split": s})
            if start:
                copy.start()
            else:
                copy.wait_send()

    def image_cell(i):
        b = (mb + i) % FC
        lanes = pl.ds(pl.multiple_of(b * W, W), W)
        pieces = [radj[b * FR + a] for a in range(FR)]
        main = jnp.concatenate(pieces, axis=0) if FR > 1 else pieces[0]
        upd = pre[:, lanes] - primal_step * (main.astype(f32) + dot(st, spill[:, lanes]))
        nb = jnp.maximum(upd, 0.0).astype(bf16)
        eb = (2.0 * nb.astype(f32) - x[b].astype(f32)).astype(bf16)
        new[b] = nb
        for a in range(FR):
            ext[b * FR + a] = eb[a * R : (a + 1) * R]
        deliver(ext, rmain, send_e, recv_e, i, True)

    def image_sides(i):
        b = (mb + i) % FC
        left = jnp.where(b > 0, take_left, 0.0).astype(bf16)
        right = jnp.where(b < FC - 1, take_right, 0.0).astype(bf16)
        nt = (((1,), (1,)), ((), ()))
        for a in range(FR):
            lf = (b + FC - 1) % FC * FR + a
            rf = (b + 1) % FC * FR + a
            both = lax.dot_general(left, ext[lf], nt, preferred_element_type=f32)
            both = both + lax.dot_general(right, ext[rf], nt, preferred_element_type=f32)
            exts[b * FR + a] = both.astype(bf16)
        deliver(exts, rsides, send_es, recv_es, i, True)

    for i in range(FC):
        image_cell(i)
        if i >= 2:
            image_sides(i - 1)
    image_sides(FC - 1)
    image_sides(0)
    forward_tables(W, B, row_taps, col_taps, fcols, frows)
    forward_cols(R, W, me, rmain, rsides, fcols, ic)
    for i in range(FC):
        for j in range(FR):
            r = i * FR + j
            if r == 0:
                continue
            src_b, src_a = (mb + FC - i) % FC, (ma + FR - j) % FR
            c = src_b * FR + src_a
            device = {"chan": c, "split": s}
            remote(exts.at[c], rsides.at[c], send_es.at[r], recv_es.at[r], device).wait_recv()
            remote(ext.at[c], rmain.at[c], send_e.at[r], recv_e.at[r], device).wait_recv()
            forward_cols(R, W, c, rmain, rsides, fcols, ic)
    for i in range(FC):
        deliver(exts, rsides, send_es, recv_es, i, False)
        deliver(ext, rmain, send_e, recv_e, i, False)
    finish_h = chain(
        ic.at[:, pl.ds(R, PAD)], htop, ic.at[:, pl.ds(PAD, PAD)], hbot, send_h, recv_h
    )
    finish_h()
    ic[:, :PAD] = htop[...]
    ic[:, PAD + R :] = hbot[...]


def per_device(sky_image, dirty_image, uv_weights, dual_coeffs, support_mask, row_taps, col_taps):
    FC, FR = sky_image.shape[1], sky_image.shape[2]
    R, W = sky_image.shape[4], sky_image.shape[5]
    C = dual_coeffs.shape[1]
    npix = FC * W
    half = npix // 2
    B = min(128, R)
    RP = R + 2 * PAD
    u = dual_coeffs.reshape(NB, C, R, W)
    x = sky_image.reshape(FC, FR * R, W)
    d = dirty_image.reshape(FC, FR * R, W)
    wts = uv_weights.reshape(half, half)
    mask = support_mask.reshape(R, W)
    colT = col_dft(npix)
    vm = lambda *shape: pltpu.VMEM(shape, bf16)
    sem = lambda n: pltpu.SemaphoreType.DMA((n,))
    any_spec = pl.BlockSpec(memory_space=pl.ANY)
    smem_spec = pl.BlockSpec(memory_space=pltpu.SMEM)
    span = B + 2 * PAD
    new, ic, frows = pl.pallas_call(
        functools.partial(step_kernel, C, FC, FR, R, W, B),
        out_shape=[
            jax.ShapeDtypeStruct((FC, FR * R, W), bf16),
            jax.ShapeDtypeStruct((NB, RP, C * W), bf16),
            jax.ShapeDtypeStruct((NB, B, span), bf16),
        ],
        in_specs=[any_spec] * 5 + [smem_spec] * 2,
        scratch_shapes=[
            vm(NB, C, R, W), vm(FC, FR * R, W), vm(FC, FR * R, W),
            pltpu.VMEM((half, half), jnp.int32), vm(npix, npix),
            vm(FC * 16, FC * W), vm(NB, W, 2 * W), vm(NB, B, span), vm(W + 16, NB * W),
            vm(NB, C, PAD, W), vm(NB, C, PAD, W), vm(NB, RP, 2 * W), vm(NB, RP, W),
            vm(C, R, W), vm(C, 16, R), vm(C, R, W), vm(C, 16, R),
            *[vm(half, npix)] * 8, pltpu.VMEM((half, npix), f32),
            vm(C, R, W), vm(C, 16, R), vm(C, R, W), vm(C, 16, R),
            vm(NB, PAD, C * W), vm(NB, PAD, C * W),
            sem(2), sem(2), sem(C), sem(C), sem(C), sem(C),
            sem(C), sem(C), sem(C), sem(C), sem(4 * half // 128), sem(4 * half // 128), sem(2), sem(2), sem(5),
        ],
        compiler_params=pltpu.CompilerParams(
            collective_id=0, has_side_effects=True, vmem_limit_bytes=58 * 2**20
        ),
    )(u, x, d, wts, colT, row_taps, col_taps)

    part = FC // NB
    new_dual, new = pl.pallas_call(
        functools.partial(shrink_body, C, R, W, B),
        grid=(NB,),
        in_specs=[
            pl.BlockSpec((1, RP, C * W), lambda n: (n, 0, 0)),
            pl.BlockSpec((1, B, B + 2 * PAD), lambda n: (n, 0, 0)),
            pl.BlockSpec((1, C, R, W), lambda n: (n, 0, 0, 0)),
            pl.BlockSpec((R, W), lambda n: (0, 0)),
            pl.BlockSpec((part, FR * R, W), lambda n: (n, 0, 0)),
        ],
        out_specs=[
            pl.BlockSpec((1, C, R, W), lambda n: (n, 0, 0, 0)),
            pl.BlockSpec((part, FR * R, W), lambda n: (n, 0, 0)),
        ],
        out_shape=[
            jax.ShapeDtypeStruct((NB, C, R, W), bf16),
            jax.ShapeDtypeStruct((FC, FR * R, W), bf16),
        ],
    )(ic, frows, u, mask, new)
    return (new.reshape(sky_image.shape), new_dual.reshape(dual_coeffs.shape))


def solution(mesh):
    placed = (
        P(("cube", "chan"), None, None, "split", None, None),
        P(("cube", "chan"), None, None, "split", None, None),
        P(("cube", "chan"), "split", None),
        P(None, "cube", "chan", "split", None, None),
        P("chan", "split", None, None),
        P(),
        P(),
    )
    return jax.shard_map(
        per_device,
        mesh=mesh,
        in_specs=placed,
        out_specs=(
            P(("cube", "chan"), None, None, "split", None, None),
            P(None, "cube", "chan", "split", None, None),
        ),
        check_vma=False,
    )
```

```python
import functools
import math

import jax
import jax.numpy as jnp
import numpy as np
from jax import lax
from jax.experimental import pallas as pl
from jax.experimental.pallas import tpu as pltpu
from jax.sharding import PartitionSpec as P

NB = 4
TAPS = 17
MARGIN = 8
PAD = 16

primal_step = 0.5
dual_step = 0.5
radius = 6.0
weight_unit = 0.25
f32 = jnp.float32
bf16 = jnp.bfloat16


def dot(a, b):
    return jnp.dot(a, b, preferred_element_type=f32)


def col_dft(npix):
    half = npix // 2
    product = np.arange(npix)[:, None] * np.arange(half)[None, :] % npix
    phases = product.astype(np.float32) * np.float32(2.0 * math.pi / npix)
    factor = np.float32(1.0 / math.sqrt(npix))
    table = np.concatenate([np.cos(phases) * factor, -np.sin(phases) * factor], axis=1)
    return jnp.asarray(table.astype(jnp.bfloat16))


def bands(index, taps):
    outs = [jnp.zeros(index.shape, f32) for _ in range(NB)]
    for t in range(TAPS):
        hit = index == t
        outs = [jnp.where(hit, taps[n, t], outs[n]) for n in range(NB)]
    return [o.astype(bf16) for o in outs]


def adjoint_tables(W, B, row_taps, col_taps, gcols, hrows):
    i = lax.broadcasted_iota(jnp.int32, (W, W), 0)
    j = lax.broadcasted_iota(jnp.int32, (W, W), 1)
    side = jnp.where(j < MARGIN, j - MARGIN, W - MARGIN + j)
    main_bands = bands(j - i + MARGIN, col_taps)
    side_bands = bands(jnp.where(j < 2 * MARGIN, side - i + MARGIN, -1), col_taps)
    r = lax.broadcasted_iota(jnp.int32, (B, B + 2 * PAD), 0)
    w = lax.broadcasted_iota(jnp.int32, (B, B + 2 * PAD), 1)
    row_bands = bands(r - w + PAD + MARGIN, row_taps)
    for n in range(NB):
        gcols[n, :, :W] = main_bands[n]
        gcols[n, :, W:] = side_bands[n]
        hrows[n] = row_bands[n]


def forward_tables(W, B, row_taps, col_taps, fcols, frows):
    i = lax.broadcasted_iota(jnp.int32, (W, W), 0)
    j = lax.broadcasted_iota(jnp.int32, (W, W), 1)
    main_bands = bands(i - j + MARGIN, col_taps)
    k = lax.broadcasted_iota(jnp.int32, (2 * MARGIN, W), 0)
    jk = lax.broadcasted_iota(jnp.int32, (2 * MARGIN, W), 1)
    side = jnp.where(k < MARGIN, k - MARGIN, W - MARGIN + k)
    side_bands = bands(side - jk + MARGIN, col_taps)
    r = lax.broadcasted_iota(jnp.int32, (B, B + 2 * PAD), 0)
    w = lax.broadcasted_iota(jnp.int32, (B, B + 2 * PAD), 1)
    row_bands = bands(w - r - PAD + MARGIN, row_taps)
    for n in range(NB):
        fcols[:W, n * W : (n + 1) * W] = main_bands[n]
        fcols[W:, n * W : (n + 1) * W] = side_bands[n]
        frows[n] = row_bands[n]


def spill_table(FC, W, spill):
    span = 2 * MARGIN
    row = lax.broadcasted_iota(jnp.int32, (FC * span, FC * W), 0)
    col = lax.broadcasted_iota(jnp.int32, (FC * span, FC * W), 1)
    rb, rk = row // span, row % span
    target = jnp.where(rk >= MARGIN, (rb + 1) * W + rk - MARGIN, rb * W - MARGIN + rk)
    spill[...] = jnp.where(target == col, 1.0, 0.0).astype(bf16)


def adjoint_group(R, W, B, first, channel, u, up, lo, gcols, hrows, adj, adjs, dc, dcs, main_done, side_done):
    per = W // 16
    span = B + 2 * PAD
    mains = [gcols[n, :, :W] for n in range(NB)]
    for pair in range(0, per, 2):
        for n in range(NB):
            acc = None
            for e in range(2):
                c = channel(first + pair + e)
                shift = 16 * (pair + e)
                side = gcols[n, :, W:].astype(f32)
                side = pltpu.roll(side, shift, 1) if shift else side
                table = jnp.concatenate([mains[n], side.astype(bf16)], axis=1)
                rows = jnp.concatenate([up[n, c], u[n, c], lo[n, c]], axis=0)
                out = dot(rows, table)
                dc[n, :, e * W : (e + 1) * W] = out[:, :W].astype(bf16)
                acc = out[:, W:] if acc is None else acc + out[:, W:]
            if pair:
                dcs[n] = dcs[n] + acc.astype(bf16)
            else:
                dcs[n] = acc.astype(bf16)
        for k in range(R // B):
            out = sum(dot(hrows[n], dc[n, k * B : k * B + span]) for n in range(NB)).astype(bf16)
            adj[first + pair, k * B : k * B + B] = out[:, :W]
            adj[first + pair + 1, k * B : k * B + B] = out[:, W:]
        main_done(first + pair)
        main_done(first + pair + 1)
    for k in range(R // B):
        out = sum(dot(hrows[n], dcs[n, k * B : k * B + span]) for n in range(NB)).T.astype(bf16)
        for cc in range(per):
            adjs[first + cc, :, k * B : k * B + B] = out[cc * 16 : cc * 16 + 16]
    for cc in range(per):
        side_done(first + cc)


def half_chunk(FC, x, colT, out, lanes):
    rows = jnp.concatenate([x[b] for b in range(FC)], axis=1)
    out[:, lanes] = dot(rows, colT[:, lanes]).astype(bf16)


def table_body(s, FR, R, colT, bown, aown, aoth):
    half = FR * R
    for a in range(FR):
        own = pl.ds(pl.multiple_of((2 * a + s) * R, R), R)
        bown[a * R : (a + 1) * R] = colT[own, :]
    odd_lane = lax.broadcasted_iota(jnp.int32, (1, half), 1) % 2 == 1
    flip = jnp.where(odd_lane & (s == 1), -1.0, 1.0).astype(f32)
    odd_row = lax.broadcasted_iota(jnp.int32, (half, 1), 0) % 2 == 1
    for dst, part in ((aown, s), (aoth, 1 - s)):
        for q in range(2):
            lanes = slice(q * half, (q + 1) * half)
            if FR == 1:
                sign = jnp.where(odd_row & (part == 1), -1.0, 1.0).astype(f32)
                dst[:, lanes] = (colT[:half, lanes].astype(f32) * (sign * flip)).astype(bf16)
                continue
            pieces = [
                colT[pl.ds(pl.multiple_of((2 * a + part) * R, R), R), lanes] for a in range(FR)
            ]
            block = jnp.concatenate(pieces, axis=0)
            dst[:, lanes] = (block.astype(f32).T * flip).astype(bf16)


def stack_re_im(ref, lanes_re, lanes_im, transpose):
    re, im = ref[:, lanes_re], ref[:, lanes_im]
    if transpose:
        return jnp.concatenate([re, im], 0), jnp.concatenate([im, -re], 0)
    return jnp.concatenate([re, -im], 0), jnp.concatenate([im, re], 0)


def vis_chunk(aown, aoth, hown, hoth, wts, out, re_l, im_l):
    own_re, own_im = stack_re_im(hown, re_l, im_l, False)
    oth_re, oth_im = stack_re_im(hoth, re_l, im_l, False)
    scale = weight_unit * wts[:, re_l].astype(f32)
    re = dot(aown[...], own_re) + dot(aoth[...], oth_re)
    out[:, re_l] = (scale * re).astype(bf16)
    im = dot(aown[...], own_im) + dot(aoth[...], oth_im)
    out[:, im_l] = (scale * im).astype(bf16)


def back_chunk(s, half, bown, wown, woth, out, re_l, im_l):
    odd = lax.broadcasted_iota(jnp.int32, (half, 1), 0) % 2 == 1
    own_sign = jnp.where(odd & (s == 1), -1.0, 1.0)
    oth_sign = jnp.where(odd & (s == 0), -1.0, 1.0)
    own_re, own_im = stack_re_im(wown, re_l, im_l, True)
    oth_re, oth_im = stack_re_im(woth, re_l, im_l, True)
    re = own_sign * dot(bown[...], own_re) + oth_sign * dot(bown[...], oth_re)
    out[:, re_l] = re.astype(bf16)
    im = own_sign * dot(bown[...], own_im) + oth_sign * dot(bown[...], oth_im)
    out[:, im_l] = im.astype(bf16)


def gradient_body(FC, W, back, colT, x, d, pre):
    step = 2 * W

    @pl.loop(0, FC // 2)
    def _(j):
        lanes = pl.ds(pl.multiple_of(j * step, step), step)
        grad = lax.dot_general(
            back[...], colT[lanes, :], (((1,), (1,)), ((), ())), preferred_element_type=f32
        )
        xs = jnp.concatenate([x[2 * j], x[2 * j + 1]], axis=1).astype(f32)
        ds = jnp.concatenate([d[2 * j], d[2 * j + 1]], axis=1).astype(f32)
        pre[:, lanes] = xs - primal_step * (grad - ds)


def side_rows(FC, FR, adjs):
    st_rows = []
    for a in range(FR):
        parts = jnp.concatenate([adjs[b * FR + a] for b in range(FC)], axis=0)
        st_rows.append(parts.astype(f32).T.astype(bf16))
    return jnp.concatenate(st_rows, axis=0) if FR > 1 else st_rows[0]


def forward_cols(R, W, c, main, sides, fcols, ic):
    out = dot(main[c], fcols[:W]) + lax.dot_general(
        sides[c], fcols[W:], (((0,), (0,)), ((), ())), preferred_element_type=f32
    )
    lanes = pl.ds(pl.multiple_of(c * W, W), W)
    for n in range(NB):
        ic[n, PAD : PAD + R, lanes] = out[:, n * W : (n + 1) * W].astype(bf16)


def shrink_body(C, R, W, B, ic, frows, u, mask, new_in, out, new_out):
    span = B + 2 * PAD
    new_out[...] = new_in[...]
    hr = frows[0]
    for k in range(R // B):
        rows = slice(k * B, (k + 1) * B)
        keep = radius * mask[rows].astype(f32)
        coef = dot(hr, ic[0, k * B : k * B + span])
        total = None
        steps = []
        for c in range(C):
            st = u[0, c, rows].astype(f32) + dual_step * coef[:, c * W : (c + 1) * W]
            steps.append(st)
            total = st * st if total is None else total + st * st
        scale = keep / jnp.maximum(jnp.sqrt(total), radius)
        for c in range(C):
            out[0, c, rows] = (steps[c] * scale).astype(bf16)


def step_kernel(
    C, FC, FR, R, W, B,
    u_hbm, x_hbm, d_hbm, wts_hbm, colT_hbm, row_taps, col_taps,
    new, ic, frows,
    u, x, d, wts, colT, spill, gcols, hrows, fcols,
    up, lo, dc, dcs, adj, adjs, radj, radjs,
    hown, hoth, wown, woth, back, bown, aown, aoth, pre,
    ext, exts, rmain, rsides, htop, hbot,
    send_u, recv_u, send_a, recv_a, send_as, recv_as,
    send_e, recv_e, send_es, recv_es, send_p, recv_p, send_h, recv_h, load,
):
    half = FC * W // 2
    me = lax.axis_index("chan")
    s = lax.axis_index("split")
    ma, mb = me % FR, me // FR
    has_up = (ma > 0) | (s == 1)
    has_down = (ma < FR - 1) | (s == 0)
    partner = {"chan": me, "split": 1 - s}
    down_id = {"chan": (me + s) % C, "split": 1 - s}
    up_id = {"chan": (me + s + C - 1) % C, "split": 1 - s}
    per = W // 16

    def remote(src, dst, ssem, rsem, device):
        return pltpu.make_async_remote_copy(
            src_ref=src, dst_ref=dst, send_sem=ssem, recv_sem=rsem,
            device_id=device, device_id_type=pl.DeviceIdType.MESH,
        )

    loads = [
        pltpu.make_async_copy(a, b, load.at[i])
        for i, (a, b) in enumerate(
            [(u_hbm, u), (colT_hbm, colT), (x_hbm, x), (wts_hbm, wts), (d_hbm, d)]
        )
    ]
    for copy in loads:
        copy.start()
    barrier = pltpu.get_barrier_semaphore()

    @pl.loop(1, C)
    def _(i):
        pl.semaphore_signal(
            barrier, inc=1, device_id={"chan": (me + i) % C, "split": s},
            device_id_type=pl.DeviceIdType.MESH,
        )

    pl.semaphore_signal(barrier, inc=1, device_id=partner, device_id_type=pl.DeviceIdType.MESH)
    if FR > 1:
        cross = jnp.where(s == 0, ma > 0, ma < FR - 1)
        cross_chan = jnp.where(s == 0, (me + C - 1) % C, (me + 1) % C)

        @pl.when(cross)
        def _():
            pl.semaphore_signal(
                barrier, inc=1, device_id={"chan": cross_chan, "split": 1 - s},
                device_id_type=pl.DeviceIdType.MESH,
            )
            pl.semaphore_wait(barrier, 1)

    adjoint_tables(W, B, row_taps, col_taps, gcols, hrows)
    loads[0].wait()
    pl.semaphore_wait(barrier, C)

    def chain(down_src, down_dst, up_src, up_dst, ssem, rsem):
        downward = remote(down_src, down_dst, ssem.at[0], rsem.at[0], down_id)
        upward = remote(up_src, up_dst, ssem.at[1], rsem.at[1], up_id)

        @pl.when(has_down)
        def _():
            downward.start()

        @pl.when(has_up)
        def _():
            upward.start()

        @pl.when(jnp.logical_not(has_up))
        def _():
            down_dst[...] = jnp.zeros_like(down_dst)

        @pl.when(jnp.logical_not(has_down))
        def _():
            up_dst[...] = jnp.zeros_like(up_dst)

        def finish():
            @pl.when(has_down)
            def _():
                downward.wait_send()
                upward.wait_recv()

            @pl.when(has_up)
            def _():
                upward.wait_send()
                downward.wait_recv()

        return finish

    finish_u = chain(u.at[:, :, pl.ds(R - PAD, PAD)], up, u.at[:, :, pl.ds(0, PAD)], lo, send_u, recv_u)
    loads[1].wait()
    table_body(s, FR, R, colT, bown, aown, aoth)
    finish_u()

    def peer(i):
        return (me + C // 2 + (i + 1) // 2 * (1 - 2 * (i % 2))) % C

    def send(buf, dst, ssem, rsem):
        def start(i):
            @pl.when(i < C - 1)
            def _():
                remote(
                    buf.at[i], dst.at[me], ssem.at[i], rsem.at[i], {"chan": peer(i), "split": s}
                ).start()

            @pl.when(i == C - 1)
            def _():
                dst[me] = buf[i]

        return start

    def finish(buf, dst, ssem, rsem):
        @pl.loop(0, C - 1)
        def _(i):
            remote(
                buf.at[i], dst.at[me], ssem.at[i], rsem.at[i], {"chan": peer(i), "split": s}
            ).wait()

    @pl.loop(0, C // per)
    def _(g):
        adjoint_group(
            R, W, B, g * per, peer, u, up, lo, gcols, hrows, adj, adjs, dc, dcs,
            send(adj, radj, send_a, recv_a), send(adjs, radjs, send_as, recv_as),
        )

    for copy in loads[2:]:
        copy.wait()
    step = 256
    chunks = half // step

    def to_partner(buf, dst, lanes, i):
        return remote(buf.at[:, lanes], dst.at[:, lanes], send_p.at[i], recv_p.at[i], partner)

    def parts(j):
        return pl.ds(j * step, step), pl.ds(half + j * step, step)

    copies = []
    for j in range(chunks):
        for q, lanes in enumerate(parts(j)):
            half_chunk(FC, x, colT, hown, lanes)
            copy = to_partner(hown, hoth, lanes, 2 * j + q)
            copy.start()
            copies.append(copy)
    spill_table(FC, W, spill)
    second = []
    for j in range(chunks):
        copies[2 * j].wait()
        copies[2 * j + 1].wait()
        vis_chunk(aown, aoth, hown, hoth, wts, wown, *parts(j))
        for q, lanes in enumerate(parts(j)):
            copy = to_partner(wown, woth, lanes, 2 * chunks + 2 * j + q)
            copy.start()
            second.append(copy)
    for j in range(chunks):
        second[2 * j].wait()
        second[2 * j + 1].wait()
        back_chunk(s, half, bown, wown, woth, back, *parts(j))
    gradient_body(FC, W, back, colT, x, d, pre)

    finish(adjs, radjs, send_as, recv_as)
    finish(adj, radj, send_a, recv_a)
    st = side_rows(FC, FR, radjs)
    k = lax.broadcasted_iota(jnp.int32, (2 * MARGIN, W), 0)
    col = lax.broadcasted_iota(jnp.int32, (2 * MARGIN, W), 1)
    take_left = jnp.where((k < MARGIN) & (col == W - MARGIN + k), 1.0, 0.0)
    take_right = jnp.where((k >= MARGIN) & (col == k - MARGIN), 1.0, 0.0)

    def deliver(buf, dst, ssem, rsem, i, start):
        b = (mb + i) % FC
        for j in range(FR):
            f = b * FR + (ma + j) % FR
            r = i * FR + j
            if r == 0:
                if start:
                    dst[me] = buf[f]
                continue
            copy = remote(buf.at[f], dst.at[me], ssem.at[r], rsem.at[r], {"chan": f, "split": s})
            if start:
                copy.start()
            else:
                copy.wait_send()

    def image_cell(i):
        b = (mb + i) % FC
        lanes = pl.ds(pl.multiple_of(b * W, W), W)
        pieces = [radj[b * FR + a] for a in range(FR)]
        main = jnp.concatenate(pieces, axis=0) if FR > 1 else pieces[0]
        upd = pre[:, lanes] - primal_step * (main.astype(f32) + dot(st, spill[:, lanes]))
        nb = jnp.maximum(upd, 0.0).astype(bf16)
        eb = (2.0 * nb.astype(f32) - x[b].astype(f32)).astype(bf16)
        new[b] = nb
        for a in range(FR):
            ext[b * FR + a] = eb[a * R : (a + 1) * R]
        deliver(ext, rmain, send_e, recv_e, i, True)

    def image_sides(i):
        b = (mb + i) % FC
        left = jnp.where(b > 0, take_left, 0.0).astype(bf16)
        right = jnp.where(b < FC - 1, take_right, 0.0).astype(bf16)
        nt = (((1,), (1,)), ((), ()))
        for a in range(FR):
            lf = (b + FC - 1) % FC * FR + a
            rf = (b + 1) % FC * FR + a
            both = lax.dot_general(left, ext[lf], nt, preferred_element_type=f32)
            both = both + lax.dot_general(right, ext[rf], nt, preferred_element_type=f32)
            exts[b * FR + a] = both.astype(bf16)
        deliver(exts, rsides, send_es, recv_es, i, True)

    order = [FC // 2 + (i + 1) // 2 * (1 - 2 * (i % 2)) for i in range(FC)]
    ready, sided = set(), set()
    for i in order:
        image_cell(i)
        ready.add(i)
        for k in order:
            if k not in sided and {(k + 1) % FC, (k - 1) % FC} <= ready:
                image_sides(k)
                sided.add(k)
    forward_tables(W, B, row_taps, col_taps, fcols, frows)
    forward_cols(R, W, me, rmain, rsides, fcols, ic)
    for i in order:
        for j in range(FR):
            r = i * FR + j
            if r == 0:
                continue
            src_b, src_a = (mb + FC - i) % FC, (ma + FR - j) % FR
            c = src_b * FR + src_a
            device = {"chan": c, "split": s}
            remote(exts.at[c], rsides.at[c], send_es.at[r], recv_es.at[r], device).wait_recv()
            remote(ext.at[c], rmain.at[c], send_e.at[r], recv_e.at[r], device).wait_recv()
            forward_cols(R, W, c, rmain, rsides, fcols, ic)
    for i in range(FC):
        deliver(exts, rsides, send_es, recv_es, i, False)
        deliver(ext, rmain, send_e, recv_e, i, False)
    finish_h = chain(
        ic.at[:, pl.ds(R, PAD)], htop, ic.at[:, pl.ds(PAD, PAD)], hbot, send_h, recv_h
    )
    finish_h()
    ic[:, :PAD] = htop[...]
    ic[:, PAD + R :] = hbot[...]


def per_device(sky_image, dirty_image, uv_weights, dual_coeffs, support_mask, row_taps, col_taps):
    FC, FR = sky_image.shape[1], sky_image.shape[2]
    R, W = sky_image.shape[4], sky_image.shape[5]
    C = dual_coeffs.shape[1]
    npix = FC * W
    half = npix // 2
    B = min(128, R)
    RP = R + 2 * PAD
    u = dual_coeffs.reshape(NB, C, R, W)
    x = sky_image.reshape(FC, FR * R, W)
    d = dirty_image.reshape(FC, FR * R, W)
    wts = uv_weights.reshape(half, half)
    mask = support_mask.reshape(R, W)
    colT = col_dft(npix)
    vm = lambda *shape: pltpu.VMEM(shape, bf16)
    sem = lambda n: pltpu.SemaphoreType.DMA((n,))
    any_spec = pl.BlockSpec(memory_space=pl.ANY)
    smem_spec = pl.BlockSpec(memory_space=pltpu.SMEM)
    span = B + 2 * PAD
    new, ic, frows = pl.pallas_call(
        functools.partial(step_kernel, C, FC, FR, R, W, B),
        out_shape=[
            jax.ShapeDtypeStruct((FC, FR * R, W), bf16),
            jax.ShapeDtypeStruct((NB, RP, C * W), bf16),
            jax.ShapeDtypeStruct((NB, B, span), bf16),
        ],
        in_specs=[any_spec] * 5 + [smem_spec] * 2,
        scratch_shapes=[
            vm(NB, C, R, W), vm(FC, FR * R, W), vm(FC, FR * R, W),
            pltpu.VMEM((half, half), jnp.int32), vm(npix, npix),
            vm(FC * 16, FC * W), vm(NB, W, 2 * W), vm(NB, B, span), vm(W + 16, NB * W),
            vm(NB, C, PAD, W), vm(NB, C, PAD, W), vm(NB, RP, 2 * W), vm(NB, RP, W),
            vm(C, R, W), vm(C, 16, R), vm(C, R, W), vm(C, 16, R),
            *[vm(half, npix)] * 8, pltpu.VMEM((half, npix), f32),
            vm(C, R, W), vm(C, 16, R), vm(C, R, W), vm(C, 16, R),
            vm(NB, PAD, C * W), vm(NB, PAD, C * W),
            sem(2), sem(2), sem(C), sem(C), sem(C), sem(C),
            sem(C), sem(C), sem(C), sem(C), sem(4 * half // 128), sem(4 * half // 128), sem(2), sem(2), sem(5),
        ],
        compiler_params=pltpu.CompilerParams(
            collective_id=0, has_side_effects=True, vmem_limit_bytes=58 * 2**20
        ),
    )(u, x, d, wts, colT, row_taps, col_taps)

    part = FC // NB
    new_dual, new = pl.pallas_call(
        functools.partial(shrink_body, C, R, W, B),
        grid=(NB,),
        in_specs=[
            pl.BlockSpec((1, RP, C * W), lambda n: (n, 0, 0)),
            pl.BlockSpec((1, B, B + 2 * PAD), lambda n: (n, 0, 0)),
            pl.BlockSpec((1, C, R, W), lambda n: (n, 0, 0, 0)),
            pl.BlockSpec((R, W), lambda n: (0, 0)),
            pl.BlockSpec((part, FR * R, W), lambda n: (n, 0, 0)),
        ],
        out_specs=[
            pl.BlockSpec((1, C, R, W), lambda n: (n, 0, 0, 0)),
            pl.BlockSpec((part, FR * R, W), lambda n: (n, 0, 0)),
        ],
        out_shape=[
            jax.ShapeDtypeStruct((NB, C, R, W), bf16),
            jax.ShapeDtypeStruct((FC, FR * R, W), bf16),
        ],
    )(ic, frows, u, mask, new)
    return (new.reshape(sky_image.shape), new_dual.reshape(dual_coeffs.shape))


def solution(mesh):
    placed = (
        P(("cube", "chan"), None, None, "split", None, None),
        P(("cube", "chan"), None, None, "split", None, None),
        P(("cube", "chan"), "split", None),
        P(None, "cube", "chan", "split", None, None),
        P("chan", "split", None, None),
        P(),
        P(),
    )
    return jax.shard_map(
        per_device,
        mesh=mesh,
        in_specs=placed,
        out_specs=(
            P(("cube", "chan"), None, None, "split", None, None),
            P(None, "cube", "chan", "split", None, None),
        ),
        check_vma=False,
    )
```
